32 devices in a mesh: groups: 2 (over x), tracks: 8 (over z, y), frames: 2 (over core).
Axes of the slice: x: 2, y: 2, z: 4, core: 2. Of those that a mesh axis runs over, the one named last changes fastest.
Arguments:
- tokens: bfloat16 [256, 256, 384], P(('groups', 'tracks'), 'frames'), parts along dimension 0, may hold values from -6 to 6
- first_frame: int32 [256], P(('groups', 'tracks')), parts along dimension 0, may hold values from 0 to 127
- visible: int32 [256, 256], P(('groups', 'tracks')), parts along dimension 0, may hold values 0 or 1
- time_qkv: bfloat16 [384, 1152], replicated, may hold values from -0.3125 to 0.3125
- time_output: bfloat16 [384, 384], replicated, may hold values from -0.3125 to 0.3125
- expand: bfloat16 [384, 1536], replicated, may hold values from -0.3125 to 0.3125
- shrink: bfloat16 [1536, 384], replicated, may hold values from -0.15625 to 0.15625
- virtual_init: bfloat16 [64, 384], replicated, may hold values from -6 to 6
- cross_query: bfloat16 [384, 384], replicated, may hold values from -0.3125 to 0.3125
- cross_kv: bfloat16 [384, 768], replicated, may hold values from -0.3125 to 0.3125
- cross_output: bfloat16 [384, 384], replicated, may hold values from -1.25 to 1.25
- self_qkv: bfloat16 [384, 1152], replicated, may hold values from -0.3125 to 0.3125
- self_output: bfloat16 [384, 384], replicated, may hold values from -0.625 to 0.625
- back_query: bfloat16 [384, 384], replicated, may hold values from -0.3125 to 0.3125
- back_kv: bfloat16 [384, 768], replicated, may hold values from -0.3125 to 0.3125
- back_output: bfloat16 [384, 384], replicated, may hold values from -1.25 to 1.25
Outputs:
- tracked: bfloat16 [256, 256, 384], P(('groups', 'tracks'), 'frames'), parts along dimension 0
The draws below stay inside these ranges and needn't reach their ends.
There are 2 independent parts, one for each index of `groups`. The reference program is written for one: setup_inputs(seed, part) draws one part's arguments, and reference() takes and returns one part's arrays. A program takes and returns all parts, laid end to end along the dimension named above; an argument that names none is the same for every part. Nothing has to cross between parts.
Inputs may be any that keep to these rules, and one draw needn't show every extreme that they name: `first_frame`: each track's first frame.
All inputs are finite; a program needn't handle non-finite values. No bound on the sum of `visible` on one device may be relied on, other than what follows from the above.
Results may differ from the reference program's by a relative error of at most 0.0095.
Values may be sent and summed in bfloat16 or wider, within the bound.
A program may use at most 128 MiB of HBM per device.

```python
import jax
import jax.numpy as jnp
from jax import lax

D = 384
FF = 1536
HEADS = 8
VIRT = 64
HEAD = 48
TRK_DEV = 16
FRM_DEV = 128
TRACKS = 128
FRAMES = 256
N_TRACKS = 8
N_FRAMES = 2


def touch_ends(drawn, rng, smallest, high):
    spot = [jax.random.randint(jax.random.fold_in(rng, axis), (), 0, length) for axis, length in enumerate(drawn.shape)]
    main_axis = drawn.shape.index(max(drawn.shape))
    next_to = spot[:main_axis] + [(spot[main_axis] + 1) % drawn.shape[main_axis]] + spot[main_axis + 1:]
    return drawn.at[tuple(spot)].set(smallest).at[tuple(next_to)].set(high)


def steps_of(stream_key, shape, cuts, smallest, high):
    def one(dim, shards_of):
        steps = jax.random.uniform(jax.random.fold_in(jax.random.fold_in(stream_key, 6), dim), (shards_of,), jnp.float32, smallest / len(cuts), high / len(cuts))
        return jnp.repeat(jnp.exp(steps), shape[dim] // shards_of).reshape((-1,) + (1,) * (len(shape) - dim - 1))

    level = one(*cuts[0])
    for cut in cuts[1:]:
        level = level * one(*cut)
    return level


def gaussian(stream_key, dims, width, most, cuts=(), kind=jnp.bfloat16):
    factor_of = steps_of(stream_key, dims, cuts, -0.22, 0.18) if cuts else 1.0
    array = jax.random.normal(stream_key, dims, jnp.float32) * width * factor_of
    return jnp.minimum(jnp.maximum(array, -most), most).astype(kind)


def setup_inputs(seed: int = 0, part: int = 0) -> dict:
    keys = jax.random.split(jax.random.key(seed), 17)
    own_keys = jax.random.split(jax.random.fold_in(keys[16], part), 17)
    tokens = gaussian(own_keys[0], (TRACKS, FRAMES, D), 1.0, 6.0, ((0, 8), (1, 2)))
    first_frame = touch_ends(jax.random.randint(own_keys[1], (TRACKS,), 0, FRAMES // 2), jax.random.fold_in(own_keys[1], 1), 0, (FRAMES // 2) - 1).astype(jnp.int32)
    visible = touch_ends((jax.random.randint(own_keys[2], (TRACKS, FRAMES), 0, 4) < 3).astype(jnp.int32), jax.random.fold_in(own_keys[2], 1), 0, 1)
    time_qkv = gaussian(keys[3], (D, 3 * D), D ** -0.5, 0.3125)
    time_output = gaussian(keys[4], (D, D), D ** -0.5, 0.3125)
    expand = gaussian(keys[5], (D, FF), D ** -0.5, 0.3125)
    shrink = gaussian(keys[6], (FF, D), FF ** -0.5, 0.15625)
    virtual_init = gaussian(keys[7], (VIRT, D), 1.0, 6.0)
    cross_query = gaussian(keys[8], (D, D), D ** -0.5, 0.3125)
    cross_kv = gaussian(keys[9], (D, 2 * D), D ** -0.5, 0.3125)
    cross_output = gaussian(keys[10], (D, D), (D // 16) ** -0.5, 1.25)
    self_qkv = gaussian(keys[11], (D, 3 * D), D ** -0.5, 0.3125)
    self_output = gaussian(keys[12], (D, D), (D // 4) ** -0.5, 0.625)
    back_query = gaussian(keys[13], (D, D), D ** -0.5, 0.3125)
    back_kv = gaussian(keys[14], (D, 2 * D), D ** -0.5, 0.3125)
    back_output = gaussian(keys[15], (D, D), (D // 16) ** -0.5, 1.25)
    return {"tokens": tokens, "first_frame": first_frame, "visible": visible, "time_qkv": time_qkv, "time_output": time_output, "expand": expand, "shrink": shrink, "virtual_init": virtual_init, "cross_query": cross_query, "cross_kv": cross_kv, "cross_output": cross_output, "self_qkv": self_qkv, "self_output": self_output, "back_query": back_query, "back_kv": back_kv, "back_output": back_output}


def normed(values):
    values = values.astype(jnp.float32)
    return values * lax.rsqrt(lax.optimization_barrier(jnp.mean(values * values, axis=-1, keepdims=True)) + 1e-06)

def product(pattern, first_operand, second_operand):
    return jnp.einsum(pattern, first_operand.astype(jnp.float32), second_operand.astype(jnp.float32))

def split_heads(values):
    return values.reshape(values.shape[:-1] + (HEADS, HEAD))

def merge_heads(values):
    return values.reshape(values.shape[:-2] + (D,))

def usable_keys(first_frame, visible, offset, length):
    frames = offset + jnp.arange(length, dtype=jnp.int32)
    seen = lax.dynamic_slice_in_dim(visible, offset, length, 1)
    return (frames[None, :] >= first_frame[:, None]) & ((seen == 1) | (frames[None, :] == first_frame[:, None]))

def time_project(tokens, time_qkv):
    projected = product('ntd,dk->ntk', normed(tokens).astype(jnp.bfloat16), time_qkv)
    time_query = normed(projected[..., :D]).astype(jnp.bfloat16)
    time_key = normed(projected[..., D:2 * D]).astype(jnp.bfloat16)
    time_value = projected[..., 2 * D:].astype(jnp.bfloat16)
    return (time_query, time_key, time_value)

def time_terms(time_query, key_piece, value_piece, usable):
    scores = product('nqhe,nkhe->nhqk', split_heads(time_query), split_heads(key_piece)) * HEAD ** (-0.5)
    weights = (jnp.exp(scores) * usable[:, None, None, :].astype(jnp.float32)).astype(jnp.bfloat16)
    numerator = product('nhqk,nkhe->nqhe', weights, split_heads(value_piece))
    denominator = jnp.transpose(lax.optimization_barrier(jnp.sum(weights.astype(jnp.float32), axis=-1)), (0, 2, 1))
    return (numerator, denominator)

def time_finish(tokens, numerator, denominator, time_output, expand, shrink):
    time_mixed = merge_heads(numerator / denominator[..., None]).astype(jnp.bfloat16)
    middle = tokens.astype(jnp.float32) + product('ntd,dk->ntk', time_mixed, time_output)
    middle_norm = normed(middle).astype(jnp.bfloat16)
    hidden = jax.nn.gelu(product('ntd,df->ntf', middle_norm, expand), approximate=True).astype(jnp.bfloat16)
    return (middle + product('ntf,fd->ntd', hidden, shrink)).astype(jnp.bfloat16)

def attend_pair(query, key, value, query_form, value_form):
    weights = jnp.exp(product(query_form, split_heads(query), split_heads(key)) * HEAD ** (-0.5)).astype(jnp.bfloat16)
    numerator = product(value_form, weights, split_heads(value))
    return (weights, numerator)

def virtual_block(settled, virtual_init, cross_query, cross_kv, cross_output, self_qkv, self_output, back_query, back_kv, back_output):
    settled_norm = normed(settled).astype(jnp.bfloat16)
    crossed = product('nfd,dk->nfk', settled_norm, cross_kv)
    track_key = normed(crossed[..., :D]).astype(jnp.bfloat16)
    track_value = crossed[..., D:].astype(jnp.bfloat16)
    virtual_norm = normed(virtual_init).astype(jnp.bfloat16)
    virtual_query = normed(product('jd,dk->jk', virtual_norm, cross_query)).astype(jnp.bfloat16)
    cross_weight, numerator = attend_pair(virtual_query, track_key, track_value, 'jhe,nfhe->fhjn', 'fhjn,nfhe->fjhe')
    totals = jnp.transpose(lax.optimization_barrier(jnp.sum(cross_weight.astype(jnp.float32), axis=-1)), (0, 2, 1))
    cross_mixed = merge_heads(numerator / totals[..., None]).astype(jnp.bfloat16)
    virtual_first = virtual_init.astype(jnp.float32)[None] + product('fjd,dk->fjk', cross_mixed, cross_output)
    selfed = product('fjd,dk->fjk', normed(virtual_first).astype(jnp.bfloat16), self_qkv)
    self_query = normed(selfed[..., :D]).astype(jnp.bfloat16)
    self_key = normed(selfed[..., D:2 * D]).astype(jnp.bfloat16)
    self_value = selfed[..., 2 * D:].astype(jnp.bfloat16)
    self_weight, numerator = attend_pair(self_query, self_key, self_value, 'fjhe,fihe->fhji', 'fhji,fihe->fjhe')
    totals = jnp.transpose(lax.optimization_barrier(jnp.sum(self_weight.astype(jnp.float32), axis=-1)), (0, 2, 1))
    self_mixed = merge_heads(numerator / totals[..., None]).astype(jnp.bfloat16)
    virtual_second = virtual_first + product('fjd,dk->fjk', self_mixed, self_output)
    backed = product('fjd,dk->fjk', normed(virtual_second).astype(jnp.bfloat16), back_kv)
    virtual_key = normed(backed[..., :D]).astype(jnp.bfloat16)
    virtual_value = backed[..., D:].astype(jnp.bfloat16)
    track_query = normed(product('nfd,dk->nfk', settled_norm, back_query)).astype(jnp.bfloat16)
    back_weight, numerator = attend_pair(track_query, virtual_key, virtual_value, 'nfhe,fjhe->nfhj', 'nfhj,fjhe->nfhe')
    totals = lax.optimization_barrier(jnp.sum(back_weight.astype(jnp.float32), axis=-1))
    back_mixed = merge_heads(numerator / totals[..., None]).astype(jnp.bfloat16)
    return (settled.astype(jnp.float32) + product('nfd,dk->nfk', back_mixed, back_output)).astype(jnp.bfloat16)

def reference(tokens, first_frame, visible, time_qkv, time_output, expand, shrink, virtual_init, cross_query, cross_kv, cross_output, self_qkv, self_output, back_query, back_kv, back_output):
    track_block = TRK_DEV // N_FRAMES
    blocks = TRACKS // track_block

    def time_part(grouped):
        time_query, time_key, time_value = time_project(grouped[0], time_qkv)
        usable = usable_keys(grouped[1], grouped[2], 0, FRAMES)
        numerator, denominator = time_terms(time_query, time_key, time_value, usable)
        return time_finish(grouped[0], numerator, denominator, time_output, expand, shrink)
    settled = lax.map(time_part, (tokens.reshape(blocks, track_block, FRAMES, D), first_frame.reshape(blocks, track_block), visible.reshape(blocks, track_block, FRAMES)))
    settled = settled.reshape(TRACKS, FRAMES, D)
    frame_block = FRM_DEV // N_TRACKS
    pieces = jnp.transpose(settled.reshape(TRACKS, FRAMES // frame_block, frame_block, D), (1, 0, 2, 3))

    def virtual_part(section):
        return virtual_block(section, virtual_init, cross_query, cross_kv, cross_output, self_qkv, self_output, back_query, back_kv, back_output)
    tracked = lax.map(virtual_part, pieces)
    return jnp.transpose(tracked, (1, 0, 2, 3)).reshape(TRACKS, FRAMES, D)
```

```python
import functools

import jax
import jax.numpy as jnp
from jax import lax
from jax.experimental import pallas as pl
from jax.experimental.pallas import tpu as pltpu
from jax.sharding import PartitionSpec as P

D = 384
HEADS = 8
HEAD = 48


def normed(values):
    values = values.astype(jnp.float32)
    return values * lax.rsqrt(jnp.mean(values * values, axis=-1, keepdims=True) + 1e-06)


def product(pattern, first_operand, second_operand):
    return jnp.einsum(pattern, first_operand, second_operand, preferred_element_type=jnp.float32)


def split_heads(values):
    return values.reshape(values.shape[:-1] + (HEADS, HEAD))


def merge_heads(values):
    return values.reshape(values.shape[:-2] + (D,))


def usable_keys(first_frame, visible, length):
    frames = jnp.arange(length, dtype=jnp.int32)
    return (frames[None, :] >= first_frame[:, None]) & (
        (visible == 1) | (frames[None, :] == first_frame[:, None])
    )


def time_project(tokens, time_qkv):
    projected = product("ntd,dk->ntk", normed(tokens).astype(jnp.bfloat16), time_qkv)
    time_query = normed(projected[..., :D]).astype(jnp.bfloat16)
    time_key = normed(projected[..., D : 2 * D]).astype(jnp.bfloat16)
    time_value = projected[..., 2 * D :].astype(jnp.bfloat16)
    return (time_query, time_key, time_value)


def time_terms(time_query, key_piece, value_piece, usable):
    scores = product("nqhe,nkhe->nhqk", split_heads(time_query), split_heads(key_piece)) * HEAD ** (
        -0.5
    )
    weights = (jnp.exp(scores) * usable[:, None, None, :].astype(jnp.float32)).astype(jnp.bfloat16)
    numerator = product("nhqk,nkhe->nqhe", weights, split_heads(value_piece))
    denominator = jnp.transpose(jnp.sum(weights.astype(jnp.float32), axis=-1), (0, 2, 1))
    return (numerator, denominator)


def time_finish(tokens, numerator, denominator, time_output, expand, shrink):
    time_mixed = merge_heads(numerator / denominator[..., None]).astype(jnp.bfloat16)
    middle = tokens.astype(jnp.float32) + product("ntd,dk->ntk", time_mixed, time_output)
    middle_norm = normed(middle).astype(jnp.bfloat16)
    hidden = jax.nn.gelu(product("ntd,df->ntf", middle_norm, expand), approximate=True).astype(
        jnp.bfloat16
    )
    return (middle + product("ntf,fd->ntd", hidden, shrink)).astype(jnp.bfloat16)


def track_complete(whole, first_frame, visible, time_qkv, time_output, expand, shrink):
    half_tracks = whole.shape[0]
    core_index = lax.axis_index("frames")
    own_first = lax.dynamic_slice_in_dim(first_frame, core_index * half_tracks, half_tracks, 0)
    own_visible = lax.dynamic_slice_in_dim(visible, core_index * half_tracks, half_tracks, 0)
    time_query, time_key, time_value = time_project(whole, time_qkv)
    usable = usable_keys(own_first, own_visible, whole.shape[1])
    numerator, denominator = time_terms(time_query, time_key, time_value, usable)
    return time_finish(whole, numerator, denominator, time_output, expand, shrink)


def attend_pair(query, key, value, query_form, value_form):
    weights = jnp.exp(
        product(query_form, split_heads(query), split_heads(key)) * HEAD ** (-0.5)
    ).astype(jnp.bfloat16)
    numerator = product(value_form, weights, split_heads(value))
    return (weights, numerator)


def virtual_block(
    settled,
    virtual_init,
    cross_query,
    cross_kv,
    cross_output,
    self_qkv,
    self_output,
    back_query,
    back_kv,
    back_output,
):
    settled_norm = normed(settled).astype(jnp.bfloat16)
    crossed = product("nfd,dk->nfk", settled_norm, cross_kv)
    track_key = normed(crossed[..., :D]).astype(jnp.bfloat16)
    track_value = crossed[..., D:].astype(jnp.bfloat16)
    virtual_norm = normed(virtual_init).astype(jnp.bfloat16)
    virtual_query = normed(product("jd,dk->jk", virtual_norm, cross_query)).astype(jnp.bfloat16)
    cross_weight, numerator = attend_pair(
        virtual_query, track_key, track_value, "jhe,nfhe->fhjn", "fhjn,nfhe->fjhe"
    )
    totals = jnp.transpose(jnp.sum(cross_weight.astype(jnp.float32), axis=-1), (0, 2, 1))
    cross_mixed = merge_heads(numerator / totals[..., None]).astype(jnp.bfloat16)
    virtual_first = virtual_init.astype(jnp.float32)[None] + product(
        "fjd,dk->fjk", cross_mixed, cross_output
    )
    selfed = product("fjd,dk->fjk", normed(virtual_first).astype(jnp.bfloat16), self_qkv)
    self_query = normed(selfed[..., :D]).astype(jnp.bfloat16)
    self_key = normed(selfed[..., D : 2 * D]).astype(jnp.bfloat16)
    self_value = selfed[..., 2 * D :].astype(jnp.bfloat16)
    self_weight, numerator = attend_pair(
        self_query, self_key, self_value, "fjhe,fihe->fhji", "fhji,fihe->fjhe"
    )
    totals = jnp.transpose(jnp.sum(self_weight.astype(jnp.float32), axis=-1), (0, 2, 1))
    self_mixed = merge_heads(numerator / totals[..., None]).astype(jnp.bfloat16)
    virtual_second = virtual_first + product("fjd,dk->fjk", self_mixed, self_output)
    backed = product("fjd,dk->fjk", normed(virtual_second).astype(jnp.bfloat16), back_kv)
    virtual_key = normed(backed[..., :D]).astype(jnp.bfloat16)
    virtual_value = backed[..., D:].astype(jnp.bfloat16)
    track_query = normed(product("nfd,dk->nfk", settled_norm, back_query)).astype(jnp.bfloat16)
    back_weight, numerator = attend_pair(
        track_query, virtual_key, virtual_value, "nfhe,fjhe->nfhj", "nfhj,fjhe->nfhe"
    )
    totals = jnp.sum(back_weight.astype(jnp.float32), axis=-1)
    back_mixed = merge_heads(numerator / totals[..., None]).astype(jnp.bfloat16)
    return (settled.astype(jnp.float32) + product("nfd,dk->nfk", back_mixed, back_output)).astype(
        jnp.bfloat16
    )


def per_device(
    tokens,
    first_frame,
    visible,
    time_qkv,
    time_output,
    expand,
    shrink,
    virtual_init,
    cross_query,
    cross_kv,
    cross_output,
    self_qkv,
    self_output,
    back_query,
    back_kv,
    back_output,
):
    whole = lax.all_to_all(tokens, "frames", split_axis=0, concat_axis=1, tiled=True)
    settled = track_complete(whole, first_frame, visible, time_qkv, time_output, expand, shrink)
    spread = lax.all_to_all(settled, ("tracks", "frames"), split_axis=1, concat_axis=0, tiled=True)
    joined = lax.all_to_all(
        virtual_block(
            spread,
            virtual_init,
            cross_query,
            cross_kv,
            cross_output,
            self_qkv,
            self_output,
            back_query,
            back_kv,
            back_output,
        ),
        ("tracks", "frames"),
        split_axis=0,
        concat_axis=1,
        tiled=True,
    )
    tracked = lax.all_to_all(joined, "frames", split_axis=1, concat_axis=0, tiled=True)
    return tracked


def row_scale(values):
    return lax.rsqrt(jnp.mean(values * values, axis=-1, keepdims=True) + 1e-06)


def unit(values):
    return values * row_scale(values)


def dot(first, second):
    return jnp.dot(first, second, preferred_element_type=jnp.float32)


def dot_t(first, second):
    return lax.dot_general(
        first, second, (((1,), (1,)), ((), ())), preferred_element_type=jnp.float32
    )


WIN = 256
GROUP = HEADS // 2
USED = GROUP * HEAD
SHIFT = D - WIN
STARTS = (0, SHIFT)
BASES = (0, USED - SHIFT)
SPARE = (USED, 0)
LOG2E = 1.4426950408889634
QSCALE = HEAD ** (-0.5) * LOG2E


def head_mask(group, head, rows):
    lane = lax.broadcasted_iota(jnp.int32, (rows, WIN), 1)
    low = BASES[group] + head * HEAD
    return (lane >= low) & (lane < low + HEAD)


def window(values, group):
    return values[:, STARTS[group] : STARTS[group] + WIN]


def with_ones(values, group):
    part = window(values, group)
    lane = lax.broadcasted_iota(jnp.int32, part.shape, 1)
    inside = (lane >= BASES[group]) & (lane < BASES[group] + USED)
    return jnp.where(inside, part, jnp.ones_like(part))


def join_windows(first, second):
    return jnp.concatenate(
        [first[:, :SHIFT], first[:, SHIFT:] + second[:, :SHIFT], second[:, SHIFT:]], axis=1
    )


def picked(summed, group, head):
    share = 1.0 / summed[:, SPARE[group] : SPARE[group] + 1]
    return jnp.where(head_mask(group, head, summed.shape[0]), summed * share, 0.0)


def head_stack(values, group):
    part = window(values, group)
    return jnp.concatenate(
        [
            jnp.where(head_mask(group, h, part.shape[0]), part, jnp.zeros_like(part))
            for h in range(GROUP)
        ],
        axis=0,
    )


def time_rows(x, usable, w_qkv, w_out, w_expand, w_shrink, length):
    tracks = x.shape[0] // length
    xf = x.astype(jnp.float32)
    projected = dot(unit(xf).astype(jnp.bfloat16), w_qkv[...])
    query = (unit(projected[:, :D]) * QSCALE).astype(jnp.bfloat16)
    key = unit(projected[:, D : 2 * D]).astype(jnp.bfloat16)
    value = projected[:, 2 * D :]
    mixed = []
    for n in range(tracks):
        rows = slice(n * length, (n + 1) * length)
        halves = []
        for group in range(2):
            held = (with_ones(value[rows], group) * usable[n]).astype(jnp.bfloat16)
            keys = window(key[rows], group)
            queries = window(query[rows], group)
            total = None
            for head in range(GROUP):
                own = jnp.where(head_mask(group, head, length), queries, jnp.zeros_like(queries))
                weights = jnp.exp2(dot_t(own, keys)).astype(jnp.bfloat16)
                part = picked(dot(weights, held), group, head)
                total = part if total is None else total + part
            halves.append(total)
        mixed.append(join_windows(*halves))
    mixed = jnp.concatenate(mixed, axis=0).astype(jnp.bfloat16)
    middle = xf + dot(mixed, w_out[...])
    inner = dot(unit(middle).astype(jnp.bfloat16), w_expand[...])
    half = 0.5 * inner
    bent = jnp.tanh(inner * (0.7978845608028654 + 0.035677408136300125 * (inner * inner)))
    hidden = (half + half * bent).astype(jnp.bfloat16)
    return (middle + dot(hidden, w_shrink[...])).astype(jnp.bfloat16)


def stacked_attention(queries, keys, values, ones_stack):
    nums, dens = [], []
    for group in range(2):
        weights = jnp.exp2(dot_t(window(queries, group), head_stack(keys, group))).astype(
            jnp.bfloat16
        )
        nums.append(dot(weights, head_stack(values, group)))
        dens.append(dot(weights, ones_stack[group]))
    return join_windows(*nums) / join_windows(*dens)


def frame_rows(s, query_stack, ones_stack, virtual, frames, refs):
    w_ckv, w_cout, w_sqkv, w_sout, w_bq, w_bkv, w_bout = refs
    tracks = s.shape[0] // frames
    virt = virtual.shape[0]
    sf = s.astype(jnp.float32)
    sn = unit(sf).astype(jnp.bfloat16)
    crossed = dot(sn, w_ckv[...])
    track_key = unit(crossed[:, :D]).astype(jnp.bfloat16)
    track_value = crossed[:, D:].astype(jnp.bfloat16)
    track_query = (unit(dot(sn, w_bq[...])) * QSCALE).astype(jnp.bfloat16)
    mixed = []
    for i in range(frames):
        rows = slice(i * tracks, (i + 1) * tracks)
        halves = []
        for group in range(2):
            weights = jnp.exp2(
                dot_t(query_stack[group], window(track_key[rows], group))
            ).astype(jnp.bfloat16)
            summed = dot(weights, with_ones(track_value[rows], group))
            total = None
            for head in range(GROUP):
                part = picked(summed[head * virt : (head + 1) * virt], group, head)
                total = part if total is None else total + part
            halves.append(total)
        mixed.append(join_windows(*halves))
    mixed = jnp.concatenate(mixed, axis=0).astype(jnp.bfloat16)
    first = jnp.concatenate([virtual] * frames, axis=0) + dot(mixed, w_cout[...])
    selfed = dot(unit(first).astype(jnp.bfloat16), w_sqkv[...])
    self_query = (unit(selfed[:, :D]) * QSCALE).astype(jnp.bfloat16)
    self_key = unit(selfed[:, D : 2 * D]).astype(jnp.bfloat16)
    self_value = selfed[:, 2 * D :].astype(jnp.bfloat16)
    mixed = []
    for i in range(frames):
        rows = slice(i * virt, (i + 1) * virt)
        mixed.append(
            stacked_attention(self_query[rows], self_key[rows], self_value[rows], ones_stack)
        )
    mixed = jnp.concatenate(mixed, axis=0).astype(jnp.bfloat16)
    second = first + dot(mixed, w_sout[...])
    backed = dot(unit(second).astype(jnp.bfloat16), w_bkv[...])
    virtual_key = unit(backed[:, :D]).astype(jnp.bfloat16)
    virtual_value = backed[:, D:].astype(jnp.bfloat16)
    mixed = []
    for i in range(frames):
        rows = slice(i * tracks, (i + 1) * tracks)
        cols = slice(i * virt, (i + 1) * virt)
        mixed.append(
            stacked_attention(track_query[rows], virtual_key[cols], virtual_value[cols], ones_stack)
        )
    mixed = jnp.concatenate(mixed, axis=0).astype(jnp.bfloat16)
    return (sf + dot(mixed, w_bout[...])).astype(jnp.bfloat16)


STEP_TRACKS = 2
STEP_FRAMES = 4


def layer_kernel(
    n_tracks_axis,
    n_frames_axis,
    tokens,
    first_frame,
    visible,
    w_qkv,
    w_out,
    w_expand,
    w_shrink,
    virtual_init,
    w_cq,
    w_ckv,
    w_cout,
    w_sqkv,
    w_sout,
    w_bq,
    w_bkv,
    w_bout,
    out,
    other,
    settled,
    spread,
    by_frame,
    result,
    returned,
    query_stack,
    ones_stack,
    usable,
    swap,
    pair_send,
    pair_recv,
    spread_send,
    spread_recv,
    back_send,
    back_recv,
):
    t = lax.axis_index("tracks")
    f = lax.axis_index("frames")
    group_index = lax.axis_index("groups")
    devices = n_tracks_axis * n_frames_axis
    me = t * n_frames_axis + f
    held, part, _ = tokens.shape
    mine = held // n_frames_axis
    length = part * n_frames_axis
    own_frames = length // devices
    virt = virtual_init.shape[0]

    def place(index):
        return (group_index, index // n_frames_axis, index % n_frames_axis)

    barrier = pltpu.get_barrier_semaphore()

    @pl.loop(1, devices)
    def _(k):
        pl.semaphore_signal(
            barrier,
            inc=1,
            device_id=place(lax.rem(me + k, devices)),
            device_id_type=pl.DeviceIdType.MESH,
        )

    frame_ids = lax.broadcasted_iota(jnp.int32, (held, length), 1)
    started = first_frame[...]
    flags = (frame_ids >= started) & ((visible[...] == 1) | (frame_ids == started))
    usable[...] = jnp.transpose(flags.astype(jnp.float32), (1, 0))
    row = lax.broadcasted_iota(jnp.int32, swap.shape, 0)
    col = lax.broadcasted_iota(jnp.int32, swap.shape, 1)
    matched = (row // held == col % own_frames) & (row % held == col // own_frames)
    swap[...] = jnp.where(matched, 1.0, 0.0).astype(jnp.bfloat16)
    virtual = virtual_init[...].astype(jnp.float32)
    virtual_query = unit(dot(unit(virtual).astype(jnp.bfloat16), w_cq[...])) * QSCALE
    for group in range(2):
        query_stack[group] = head_stack(virtual_query, group).astype(jnp.bfloat16)
        ones_stack[group] = jnp.concatenate(
            [
                jnp.where(head_mask(group, h, virt), 1.0, 0.0).astype(jnp.bfloat16)
                for h in range(GROUP)
            ],
            axis=0,
        )

    pl.semaphore_wait(barrier, devices - 1)

    def pair_copy(n):
        return pltpu.make_async_remote_copy(
            src_ref=tokens.at[(1 - f) * mine + n],
            dst_ref=other.at[n],
            send_sem=pair_send.at[n],
            recv_sem=pair_recv.at[n],
            device_id=(group_index, t, 1 - f),
            device_id_type=pl.DeviceIdType.MESH,
        )

    @pl.loop(0, mine)
    def _(n):
        pair_copy(n).start()

    def spread_source(index, n):
        half = lax.rem(index + f, n_frames_axis)
        base = half * part + (index // n_frames_axis) * own_frames
        return settled.at[
            pl.ds(n, STEP_TRACKS), pl.ds(pl.multiple_of(base, own_frames), own_frames), :
        ]

    @pl.loop(0, mine // STEP_TRACKS)
    def _(step):
        n0 = step * STEP_TRACKS
        pieces, flags = [], []
        lane = lax.broadcasted_iota(jnp.int32, (part, held), 1)
        for k in range(STEP_TRACKS):
            pair_copy(n0 + k).wait_recv()
            pieces.append(tokens[f * mine + n0 + k])
            pieces.append(other[n0 + k])
            chosen = lane == f * mine + n0 + k
            column = []
            for side in range(n_frames_axis):
                at = pl.multiple_of(lax.rem(f + side, n_frames_axis) * part, part)
                seen = jnp.where(chosen, usable[pl.ds(at, part), :], 0.0)
                column.append(jnp.sum(seen, axis=1, keepdims=True))
            flags.append(jnp.concatenate(column, axis=0))
        done = time_rows(
            jnp.concatenate(pieces, axis=0), flags, w_qkv, w_out, w_expand, w_shrink, length
        )
        settled[pl.ds(n0, STEP_TRACKS)] = done.reshape(STEP_TRACKS, length, D)
        dst = spread.at[pl.ds(me * mine + n0, STEP_TRACKS)]
        pltpu.make_async_copy(spread_source(me, n0), dst, spread_recv).start()

        @pl.loop(1, devices)
        def _(k):
            index = lax.rem(me + k, devices)
            pltpu.make_async_remote_copy(
                src_ref=spread_source(index, n0),
                dst_ref=dst,
                send_sem=spread_send,
                recv_sem=spread_recv,
                device_id=place(index),
                device_id_type=pl.DeviceIdType.MESH,
            ).start()

    @pl.loop(0, mine)
    def _(n):
        pair_copy(n).wait_send()

    sent = settled.at[:, pl.ds(0, length - own_frames), :]
    pltpu.make_async_copy(sent, sent, spread_send).wait()
    pltpu.make_async_copy(spread, spread, spread_recv).wait()

    @pl.loop(0, n_tracks_axis)
    def _(c):
        at = pl.multiple_of(c * held, held)
        rows = spread[pl.ds(at, held)].reshape(held * own_frames, D)
        turned = dot(swap[...], rows).astype(jnp.bfloat16)
        by_frame[:, pl.ds(at, held), :] = turned.reshape(own_frames, held, D)

    refs = (w_ckv, w_cout, w_sqkv, w_sout, w_bq, w_bkv, w_bout)
    all_tracks = held * n_tracks_axis

    @pl.loop(0, own_frames // STEP_FRAMES)
    def _(step):
        f0 = step * STEP_FRAMES
        s = by_frame[pl.ds(f0, STEP_FRAMES)].reshape(STEP_FRAMES * all_tracks, D)
        done = frame_rows(
            s, query_stack, ones_stack, virtual_init[...].astype(jnp.float32), STEP_FRAMES, refs
        )
        result[pl.ds(f0, STEP_FRAMES)] = done.reshape(STEP_FRAMES, all_tracks, D)
        dst = returned.at[t, pl.ds(f0, STEP_FRAMES)]

        def source(index):
            return result.at[
                pl.ds(f0, STEP_FRAMES), pl.ds(pl.multiple_of(index * held, held), held), :
            ]

        pltpu.make_async_copy(source(t), dst, back_recv).start()

        @pl.loop(1, n_tracks_axis)
        def _(k):
            index = lax.rem(t + k, n_tracks_axis)
            pltpu.make_async_remote_copy(
                src_ref=source(index),
                dst_ref=dst,
                send_sem=back_send,
                recv_sem=back_recv,
                device_id=(group_index, index, f),
                device_id_type=pl.DeviceIdType.MESH,
            ).start()

    sent = result.at[:, pl.ds(0, all_tracks - held), :]
    pltpu.make_async_copy(sent, sent, back_send).wait()
    pltpu.make_async_copy(returned, returned, back_recv).wait()

    @pl.loop(0, n_tracks_axis)
    def _(c):
        rows = returned[c].reshape(own_frames * held, D)
        turned = dot(swap[...], rows).astype(jnp.bfloat16)
        at = pl.multiple_of(c * own_frames, own_frames)
        out[:, pl.ds(at, own_frames), :] = turned.reshape(held, own_frames, D)


def fused_device(n_tracks_axis, n_frames_axis, tokens, first_frame, visible, *weights):
    held, part, _ = tokens.shape
    mine = held // n_frames_axis
    length = part * n_frames_axis
    own_frames = length // (n_tracks_axis * n_frames_axis)
    all_tracks = held * n_tracks_axis
    vmem = pl.BlockSpec(memory_space=pltpu.VMEM)
    virt = weights[4].shape[0]
    bf16 = jnp.bfloat16
    return pl.pallas_call(
        functools.partial(layer_kernel, n_tracks_axis, n_frames_axis),
        out_shape=jax.ShapeDtypeStruct(tokens.shape, bf16),
        in_specs=[vmem] * (3 + len(weights)),
        out_specs=vmem,
        scratch_shapes=[
            pltpu.VMEM((mine, part, D), bf16),
            pltpu.VMEM((mine, length, D), bf16),
            pltpu.VMEM((all_tracks, own_frames, D), bf16),
            pltpu.VMEM((own_frames, all_tracks, D), bf16),
            pltpu.VMEM((own_frames, all_tracks, D), bf16),
            pltpu.VMEM((n_tracks_axis, own_frames, held, D), bf16),
            pltpu.VMEM((2, GROUP * virt, WIN), bf16),
            pltpu.VMEM((2, GROUP * virt, WIN), bf16),
            pltpu.VMEM((length, held), jnp.float32),
            pltpu.VMEM((held * own_frames, held * own_frames), bf16),
            pltpu.SemaphoreType.DMA((mine,)),
            pltpu.SemaphoreType.DMA((mine,)),
            pltpu.SemaphoreType.DMA,
            pltpu.SemaphoreType.DMA,
            pltpu.SemaphoreType.DMA,
            pltpu.SemaphoreType.DMA,
        ],
        compiler_params=pltpu.CompilerParams(collective_id=0, has_side_effects=True),
    )(tokens, first_frame.reshape(held, 1), visible, *weights)


def fits(tracks_axis, frames_axis, tokens):
    held = tokens.shape[0]
    own_frames = tokens.shape[1] // tracks_axis
    return (
        frames_axis == 2
        and held % (2 * STEP_TRACKS) == 0
        and own_frames % 16 == 0
        and own_frames == held
        and tokens.shape[1] % 128 == 0
    )


def solution(mesh):
    placed = (
        P(("groups", "tracks"), "frames", None),
        P(("groups", "tracks")),
        P(("groups", "tracks"), None),
        P(),
        P(),
        P(),
        P(),
        P(),
        P(),
        P(),
        P(),
        P(),
        P(),
        P(),
        P(),
        P(),
    )
    axes = (mesh.shape["tracks"], mesh.shape["frames"])

    def body(tokens, *rest):
        if fits(*axes, tokens):
            return fused_device(*axes, tokens, *rest)
        return per_device(tokens, *rest)

    return jax.shard_map(
        body,
        mesh=mesh,
        in_specs=placed,
        out_specs=P(("groups", "tracks"), "frames", None),
        check_vma=False,
    )
```
